32 devices in a mesh: seq: 8 (over y, x, core), exp: 4 (over z).
Axes of the slice: x: 2, y: 2, z: 4, core: 2. Of those that a mesh axis runs over, the one named last changes fastest.
Arguments:
- queries: bfloat16 [1024, 2048], P('seq', 'exp'), may hold values from -10 to 10
- key_rows: bfloat16 [1024, 2048], P('seq', 'exp'), may hold values from -10 to 10
- value_rows: bfloat16 [1024, 2048], P('seq', 'exp'), may hold values from -6 to 6
- residual: bfloat16 [1024, 2048], P('seq'), may hold values from -20 to 20
- out_weight: bfloat16 [2048, 2048], P('exp'), may hold values from -1 to 1
- norm_gain: float32 [2048], replicated, may hold values from 0.5 to 1.5
- gate_weight: bfloat16 [16, 2048, 1408], P('seq', None, 'exp'), may hold values from -0.125 to 0.125
- up_weight: bfloat16 [16, 2048, 1408], P('seq', None, 'exp'), may hold values from -0.125 to 0.125
- down_weight: bfloat16 [16, 1408, 2048], P('seq', 'exp'), may hold values from -0.15625 to 0.15625
- routes: int32 [1024, 6], P('seq'), may hold values from 0 to 15, all different within a row; in each aligned block of 128 rows (0 to 127, 128 to 255, ...) at most 96 rows name the same one
- route_gates: float32 [1024, 6], P('seq'), may hold values from 0.2 to 1
- block_picks: int32 [2, 3], replicated, may hold values from 0 to 1, as said below
Outputs:
- layer_out: bfloat16 [1024, 2048], P(('seq', 'exp'))
The draws below stay inside these ranges and needn't reach their ends.
Inputs may be any that keep to these rules, and one draw needn't show every extreme that they name: `block_picks`: row b names block b first, then blocks at or before b, repeats allowed. `routes`: in each aligned block of 128 rows no expert is named by more than 96 rows, a bound that some block reaches.
All inputs are finite; a program needn't handle non-finite values.
Results may differ from the reference program's by a relative error of at most 0.015.
Values may be sent and summed in bfloat16 or wider, within the bound.
No kernel may reach another device: no remote copies, remote signals or barrier semaphores. Data moves between devices by JAX's collectives and lax.ppermute only.
A program may use at most 64 MiB of HBM per device.

```python
import math
import jax
import jax.numpy as jnp
import numpy as np
from jax import lax

D = 2048
H = 16
HD = 128
FF = 1408
TOPK = 6
BLK = 512
TOPB = 3
TOK_SEQ = 128
TOKENS = 1024
EXPERTS = 16
MOST = 96
N_SEQ = 8
N_EXP = 4


def attention_pair(key):
    base_key = jax.random.fold_in(key, 7)
    key_query, key_keys = jax.random.split(base_key, 2)
    row_width = H * HD
    query_draw = jnp.clip(jax.random.normal(key_query, (TOKENS, row_width), jnp.float32), -6.0, 6.0)
    key_draw = jnp.clip(jax.random.normal(key_keys, (TOKENS, row_width), jnp.float32), -6.0, 6.0)
    return (query_draw, key_draw)


def draw_queries(key, part):
    return attention_pair(key)[0].astype(jnp.bfloat16)


def draw_key_rows(key, part):
    return attention_pair(key)[1].astype(jnp.bfloat16)


def draw_residual(key, part):
    key_base = jax.random.fold_in(jax.random.fold_in(key, 11), 0)
    return jnp.clip(jax.random.normal(key_base, (TOKENS, D), jnp.float32), -6.0, 6.0).astype(jnp.bfloat16)


def draw_block_picks(key, part):
    nblocks = TOKENS // BLK
    own_block = jnp.arange(nblocks, dtype=jnp.int32)
    raw_draw = jax.random.randint(jax.random.fold_in(key, 13), (nblocks, TOPB - 1), 0, 1 << 20, dtype=jnp.int32)
    earlier = raw_draw % (own_block[:, None] + 1)
    return jnp.concatenate([own_block[:, None], earlier], axis=1).astype(jnp.int32)


def block_levels(key, extent, shards, low, largest):
    factor_of = 1.0
    for axis_at, shards_of in shards:
        steps = jax.random.uniform(jax.random.fold_in(jax.random.fold_in(key, 6), axis_at), (shards_of,), jnp.float32, low / len(shards), largest / len(shards))
        factor_of = factor_of * jnp.repeat(jnp.exp(steps), extent[axis_at] // shards_of).reshape((-1,) + (1,) * (len(extent) - 1 - axis_at))
    return factor_of


def shared_out(rng, own, number, rows, amount, top, most, lean):
    ranking = jax.random.permutation(rng, amount)
    packed, common = shares(amount, rows * top, most, lean, True), shares(amount, rows * top, most, lean, False)
    places = jnp.arange(amount)

    def named(sizes, offset_by):
        used = int((sizes > 0).sum())
        fixed = max(1, used // 4)
        passed = fixed + (places - fixed + offset_by * (used - fixed)) % max(1, amount - fixed)
        return jnp.zeros((amount,), jnp.int32).at[ranking[jnp.where(places < fixed, places, passed)]].set(jnp.asarray(sizes, jnp.int32))

    sizes = jnp.where(number % 4 == 0, named(packed, number // 4), named(common, number - number // 4 - 1))
    mixed = jax.random.permutation(jax.random.fold_in(own, 3), amount)
    donor, receiver = mixed[0:amount // 2 * 2:2], mixed[1:amount // 2 * 2:2]
    room = jnp.minimum(sizes[donor] - 1, most - sizes[receiver]) // 2
    room = jnp.where((donor == ranking[0]) | (receiver == ranking[0]) | (sizes[receiver] == 0), 0, jnp.maximum(room, 0))
    passed = jax.random.randint(jax.random.fold_in(own, 4), (amount // 2,), 0, 1 << 20) % (room + 1)
    sizes = sizes.at[donor].add(-passed).at[receiver].add(passed)
    labels = jnp.searchsorted(jnp.cumsum(sizes), jnp.arange(rows * top), side="right").astype(jnp.int32)
    listing = labels.reshape(top, rows).T
    listing = listing[jax.random.permutation(jax.random.fold_in(own, 1), rows)]
    offset_by = jax.random.randint(jax.random.fold_in(own, 2), (rows, 1), 0, top)
    return jnp.take_along_axis(listing, (jnp.arange(top)[None, :] + offset_by) % top, axis=1)


def shares(amount, total, reach, lean, full):
    portions = [(1 << 20) // math.isqrt(standing ** lean) + 1 for standing in range(1, amount + 1)]
    largest = reach if full else min(reach, max(-(-total // amount), total * portions[0] // sum(portions)))
    least = 1 if total - largest >= amount - 1 else 0
    given, surplus = [largest] + [least] * (amount - 1), total - largest - least * (amount - 1)
    while surplus > 0:
        movable = [i for i in range(1, amount) if given[i] < largest] or [i for i in range(1, amount) if given[i] < reach]
        pool, left = sum([portions[i] for i in movable]), surplus
        for i in movable:
            addition = min(reach - given[i], max(1, left * portions[i] // pool), surplus)
            given[i] = given[i] + addition
            surplus = surplus - addition
    return np.array(given)


def noise(key, extent, deviation, reach, shards=(), held_as=jnp.bfloat16):
    result = jax.random.normal(key, extent, jnp.float32) * deviation
    if len(shards) > 0:
        result = block_levels(key, extent, shards, -0.22, 0.18) * result
    return jnp.clip(result, min=-reach, max=reach).astype(held_as)


def setup_inputs(seed: int = 0) -> dict:
    key_list = jax.random.split(jax.random.key(seed), 13)
    queries = draw_queries(jax.random.fold_in(key_list[12], 71), 0)
    key_rows = draw_key_rows(jax.random.fold_in(key_list[12], 71), 0)
    value_rows = noise(key_list[2], (TOKENS, H * HD), 1.0, 6.0, ((0, 8), (1, 4)))
    residual = draw_residual(jax.random.fold_in(key_list[12], 71), 0)
    out_weight = noise(key_list[4], (H * HD, D), (H * HD // 64) ** -0.5, 1.0, ((0, 4),))
    norm_gain = jnp.clip(1.0 + 0.1 * jax.random.normal(key_list[5], (D,), jnp.float32), 0.5, 1.5)
    gate_weight = noise(key_list[6], (EXPERTS, D, FF), D ** -0.5, 0.125, ((0, 8), (2, 4)))
    up_weight = noise(key_list[7], (EXPERTS, D, FF), D ** -0.5, 0.125, ((0, 8), (2, 4)))
    down_weight = noise(key_list[8], (EXPERTS, FF, D), FF ** -0.5, 0.15625, ((0, 8), (1, 4)))
    routes_keys = jax.random.split(jax.random.fold_in(key_list[9], 1), TOKENS // TOK_SEQ)
    routes_turns = jax.random.permutation(jax.random.fold_in(key_list[9], 3), TOKENS // TOK_SEQ)
    routes = jax.vmap(lambda own, number: shared_out(jax.random.fold_in(key_list[9], 2), own, number, TOK_SEQ, EXPERTS, TOPK, MOST, 2))(routes_keys, routes_turns).reshape((TOKENS, TOPK))
    route_gates = jnp.clip(0.2 + 0.8 * jax.random.uniform(key_list[10], (TOKENS, TOPK), jnp.float32) ** block_levels(key_list[10], (TOKENS, TOPK), ((0, 8),), -0.2, 0.2), 0.2, 1.0)
    block_picks = draw_block_picks(jax.random.fold_in(key_list[12], 71), 0)
    return dict(queries=queries, key_rows=key_rows, value_rows=value_rows, residual=residual, out_weight=out_weight, norm_gain=norm_gain, gate_weight=gate_weight, up_weight=up_weight, down_weight=down_weight, routes=routes, route_gates=route_gates, block_picks=block_picks)


def reference(queries, key_rows, value_rows, residual, out_weight, norm_gain, gate_weight, up_weight, down_weight, routes, route_gates, block_picks):
    positions = jnp.arange(TOKENS, dtype=jnp.int32)
    nblocks = TOKENS // BLK
    block_of = positions // BLK
    chosen = jnp.any(block_picks[:, :, None] == jnp.arange(nblocks, dtype=jnp.int32)[None, None, :], axis=1)
    allowed = chosen[block_of][:, block_of] & (positions[None, :] <= positions[:, None])
    score_scale = 1.0 / math.sqrt(HD)

    def one_head(head_index):
        first_col = (head_index * HD).astype(jnp.int32)
        q_head = lax.dynamic_slice_in_dim(queries, first_col, HD, 1)
        k_head = lax.dynamic_slice_in_dim(key_rows, first_col, HD, 1)
        v_head = lax.dynamic_slice_in_dim(value_rows, first_col, HD, 1)
        scores = jnp.dot(q_head, k_head.T, preferred_element_type=jnp.float32) * score_scale
        peak = lax.optimization_barrier(jnp.max(jnp.where(allowed, scores, -1e+30), axis=1, keepdims=True))
        expo = jnp.where(allowed, jnp.exp(scores - peak), 0.0)
        totals = lax.optimization_barrier(jnp.sum(expo, axis=1, keepdims=True))
        weights = expo.astype(jnp.bfloat16)
        mixed_values = jnp.dot(weights, v_head, preferred_element_type=jnp.float32) / totals
        return mixed_values.astype(jnp.bfloat16)
    per_head = lax.map(one_head, jnp.arange(H, dtype=jnp.int32))
    attended = jnp.transpose(per_head, (1, 0, 2)).reshape(TOKENS, H * HD)
    projected = jnp.dot(attended, out_weight, preferred_element_type=jnp.float32)
    hidden_state = residual.astype(jnp.float32) + projected
    mean_square = lax.optimization_barrier(jnp.mean(hidden_state * hidden_state, axis=-1, keepdims=True))
    normed = (hidden_state * lax.rsqrt(mean_square + 1e-06) * norm_gain.astype(jnp.float32)).astype(jnp.bfloat16)
    flat_routes = routes.reshape(-1)
    flat_gates = route_gates.reshape(-1)
    capacity = N_SEQ * MOST
    slice_width = FF // N_EXP

    def add_expert(running, expert):
        expert_hits = flat_routes == expert
        picked = jnp.nonzero(expert_hits, size=capacity, fill_value=0)[0].astype(jnp.int32)
        hit_count = jnp.sum(expert_hits.astype(jnp.int32))
        live_slot = jnp.arange(capacity, dtype=jnp.int32) < hit_count
        token_ids = (picked // TOPK).astype(jnp.int32)
        token_rows = normed[token_ids]
        gate_part = jnp.dot(token_rows, gate_weight[expert], preferred_element_type=jnp.float32)
        up_part = jnp.dot(token_rows, up_weight[expert], preferred_element_type=jnp.float32)
        inner_act = (jax.nn.silu(gate_part) * up_part).astype(jnp.bfloat16)
        pieces = jnp.einsum('csf,sfd->scd', inner_act.reshape(capacity, N_EXP, slice_width).astype(jnp.float32), down_weight[expert].reshape(N_EXP, slice_width, D).astype(jnp.float32))
        rounded = lax.optimization_barrier(pieces.astype(jnp.bfloat16))
        partial_value = lax.optimization_barrier(jnp.sum(rounded.astype(jnp.float32), axis=0))
        gate_values = jnp.where(live_slot, flat_gates[picked], 0.0)
        return (running.at[token_ids].add(partial_value * gate_values[:, None]), None)
    mixture, _ = lax.scan(add_expert, jnp.zeros((TOKENS, D), jnp.float32), jnp.arange(EXPERTS, dtype=jnp.int32))
    return (hidden_state + mixture).astype(jnp.bfloat16)
```

```python
import functools

import jax
import jax.numpy as jnp
from jax import lax
from jax.experimental import pallas as pl
from jax.experimental.pallas import tpu as pltpu
from jax.sharding import PartitionSpec as P


HD = 128
BLK = 512
LANES = 128
MIB = 1 << 20
VMEM = pltpu.MemorySpace.VMEM
SMEM = pltpu.MemorySpace.SMEM
HBM = pltpu.MemorySpace.HBM


def call(kernel, out_shape, in_spaces, limit, scratch=()):
    specs = [pl.BlockSpec(memory_space=s) for s in in_spaces]
    return pl.pallas_call(
        kernel,
        out_shape=out_shape,
        in_specs=specs,
        out_specs=jax.tree.map(lambda _: pl.BlockSpec(memory_space=VMEM), out_shape),
        scratch_shapes=list(scratch),
        compiler_params=pltpu.CompilerParams(vmem_limit_bytes=limit * MIB),
    )


def xor_swap(count, mask):
    return [(i, i ^ mask) for i in range(count)]


def load_kernel(seq_count, exp_count, expert_count, picks_ref, routes_ref, gates_ref, *refs):
    copied = (len(refs) - 4) // 2
    sources, targets = refs[:copied], refs[copied : 2 * copied]
    key_out, gates_out, turned, sems = refs[2 * copied :]
    seq_index, exp_index = lax.axis_index("seq"), lax.axis_index("exp")
    top, rows = routes_ref.shape
    share = rows // exp_count
    here = pl.ds(pl.multiple_of(exp_index * share, share), share)
    copies = []
    for i in range(copied):
        source = sources[i].at[here] if i == 0 else sources[i]
        copies.append(pltpu.make_async_copy(source, targets[i], sems.at[i]))
        copies[-1].start()

    block = seq_index * rows // BLK
    lane = lax.broadcasted_iota(jnp.int32, (1, rows), 1)
    for mask in range(seq_count):
        group = seq_index ^ mask
        key_block = group * rows // BLK
        seen = picks_ref[block, 0] == key_block
        for j in range(1, picks_ref.shape[1]):
            seen = seen | (picks_ref[block, j] == key_block)
        key_out[:, mask * rows : (mask + 1) * rows] = lane + jnp.where(seen, group * rows, 1 << 30)

    width = gates_out.shape[1]
    line = lax.broadcasted_iota(jnp.int32, (width, rows), 0)
    expert = jnp.where(line < expert_count, line, line - expert_count)
    value = jnp.zeros((width, rows), jnp.float32)
    for k in range(top):
        hit = expert == routes_ref[k : k + 1, :]
        value = value + jnp.where(hit, gates_ref[k : k + 1, :], 0.0)
    high = value.astype(jnp.bfloat16).astype(jnp.float32)
    turned[...] = jnp.where(line < expert_count, high, value - high).T
    gates_out[...] = turned[here, :].astype(jnp.bfloat16)
    for copy in copies:
        copy.wait()


def attention_kernel(count, key_ref, own_ref, *refs):
    pieces, (own_out, partner_out) = refs[:count], refs[count:]
    seq_index = lax.axis_index("seq")
    rows, width = own_ref.shape
    key_pos = key_ref[...]
    line = lax.broadcasted_iota(jnp.int32, (rows, 1), 0)
    query_pos = jnp.concatenate(
        [line + seq_index * rows, line + (seq_index ^ 1) * rows], axis=0
    )
    allowed = key_pos <= query_pos
    for first in range(0, width, HD):
        q = jnp.concatenate(
            [
                own_ref[:, first : first + HD],
                pieces[1][:, 2 * width + first : 2 * width + first + HD],
            ],
            axis=0,
        )
        k = jnp.concatenate([p[:, first : first + HD] for p in pieces], axis=0)
        v = jnp.concatenate(
            [p[:, width + first : width + first + HD] for p in pieces], axis=0
        )
        scores = lax.dot_general(
            q, k, (((1,), (1,)), ((), ())), preferred_element_type=jnp.float32
        ) * (HD ** -0.5)
        scores = jnp.where(allowed, scores, -1e30)
        peak = jnp.max(scores, axis=1, keepdims=True)
        expo = jnp.where(allowed, jnp.exp(scores - peak), 0.0)
        total = jnp.sum(expo, axis=1, keepdims=True)
        mixed = jnp.dot(expo.astype(jnp.bfloat16), v, preferred_element_type=jnp.float32) / total
        mixed = mixed.astype(jnp.bfloat16)
        own_out[:, first : first + HD] = mixed[:rows]
        partner_out[:, first : first + HD] = mixed[rows:]


def project_kernel(exp_count, mine_ref, other_ref, weight_ref, own_out, *outs):
    rows, width = mine_ref.shape
    share = rows // exp_count
    exp_index = lax.axis_index("exp")
    half = lax.axis_index("seq") & 1

    def turned(ref):
        parts = []
        for r in range(exp_count):
            first = pl.multiple_of((exp_index ^ r) * share, share)
            parts.append(ref[pl.ds(first, share), :])
        return jnp.concatenate(parts, axis=0)

    first = pl.multiple_of(half * width, width)
    last = pl.multiple_of((1 - half) * width, width)
    result = jnp.dot(
        turned(mine_ref), weight_ref[pl.ds(first, width), :], preferred_element_type=jnp.float32
    ) + jnp.dot(
        turned(other_ref), weight_ref[pl.ds(last, width), :], preferred_element_type=jnp.float32
    )
    own_out[...] = result[:share]
    for r in range(1, exp_count):
        outs[r - 1][...] = result[r * share : (r + 1) * share].astype(jnp.bfloat16)


def norm_kernel(exp_count, own_ref, *refs):
    received = refs[: exp_count - 1]
    residual_ref, gain_ref, gates_ref, hidden_out, rows_out = refs[exp_count - 1 :]
    width = own_ref.shape[1]
    projected = own_ref[...]
    for r in received:
        projected = projected + r[...].astype(jnp.float32)
    hidden = residual_ref[...].astype(jnp.float32) + projected
    mean_square = jnp.mean(hidden * hidden, axis=-1, keepdims=True)
    hidden_out[...] = hidden
    rows_out[:, :width] = (hidden * lax.rsqrt(mean_square + 1e-06) * gain_ref[...]).astype(
        jnp.bfloat16
    )
    rows_out[:, width:] = gates_ref[...]


def expert_kernel(expert_count, local, arrays, *refs):
    pieces = refs[:arrays]
    gate_ref, up_ref, down_ref = refs[arrays : arrays + 3]
    outs = refs[arrays + 3 :]
    rows = pieces[0].shape[1]
    inner_width, width = down_ref.shape
    hidden_units = inner_width // local
    places = [(p, i) for p in pieces for i in range(p.shape[0])]
    tokens = jnp.concatenate([p[i, :, :width] for p, i in places], axis=0)
    gates = jnp.concatenate([p[i, :, width:] for p, i in places], axis=0)
    gates = gates.astype(jnp.float32)
    line = lax.broadcasted_iota(jnp.int32, (1, gates.shape[1]), 1)
    column = lax.broadcasted_iota(jnp.int32, (1, inner_width), 1)
    scale = jnp.zeros((gates.shape[0], inner_width), jnp.float32)
    for e in range(local):
        expert = lax.axis_index("seq") * local + e
        chosen = (line == expert) | (line == expert + expert_count)
        value = jnp.sum(jnp.where(chosen, gates, 0.0), axis=1, keepdims=True)
        here = (column >= e * hidden_units) & (column < (e + 1) * hidden_units)
        scale = jnp.where(here, value, scale)
    turn = (((1,), (1,)), ((), ()))
    gate = lax.dot_general(tokens, gate_ref[...], turn, preferred_element_type=jnp.float32)
    up = lax.dot_general(tokens, up_ref[...], turn, preferred_element_type=jnp.float32)
    inner = (gate / (1.0 + jnp.exp(-gate)) * up * scale).astype(jnp.bfloat16)
    result = jnp.dot(inner, down_ref[...], preferred_element_type=jnp.float32)
    at = 0
    for out in outs:
        for i in range(out.shape[0]):
            out[i] = result[at : at + rows].astype(jnp.bfloat16)
            at += rows


def join_kernel(a_ref, b_ref, out_ref):
    out_ref[: a_ref.shape[0]] = a_ref[...]
    out_ref[a_ref.shape[0] :] = b_ref[...]


def join(a, b):
    shape = jax.ShapeDtypeStruct((a.shape[0] + b.shape[0],) + a.shape[1:], a.dtype)
    return call(join_kernel, shape, [VMEM] * 2, 8)(a, b)


def plus_kernel(a_ref, b_ref, *outs):
    at = 0
    for out in outs:
        part = slice(at, at + out.shape[0])
        at += out.shape[0]
        out[...] = (a_ref[part].astype(jnp.float32) + b_ref[part].astype(jnp.float32)).astype(
            out.dtype
        )


def plus(a, b, parts=1):
    shape = jax.ShapeDtypeStruct((a.shape[0] // parts,) + a.shape[1:], a.dtype)
    return call(plus_kernel, (shape,) * parts, [VMEM] * 2, 8)(a, b)


def per_device(
    queries,
    key_rows,
    value_rows,
    residual,
    out_weight,
    norm_gain,
    gate_weight,
    up_weight,
    down_weight,
    routes,
    route_gates,
    block_picks,
):
    seq_count = lax.axis_size("seq")
    exp_count = lax.axis_size("exp")
    seq_index = lax.axis_index("seq")
    tok_rows, head_width = queries.shape
    width = residual.shape[1]
    share = tok_rows // exp_count
    local, _, hidden_units = gate_weight.shape
    expert_count = local * seq_count
    half_width = head_width // 2
    core = seq_index & 1
    bf16, f32 = jnp.bfloat16, jnp.float32

    def seq_send(a, mask):
        return lax.ppermute(a, "seq", xor_swap(seq_count, mask))

    def exp_send(a, by):
        return lax.ppermute(a, "exp", xor_swap(exp_count, by))

    def half_of(a, which):
        return lax.dynamic_slice_in_dim(a, which * half_width, half_width, 1)

    kv_same = jnp.concatenate([half_of(key_rows, core), half_of(value_rows, core)], axis=1)
    other = [half_of(a, 1 - core) for a in (key_rows, value_rows, queries)]
    kv_other = jnp.concatenate(other[:2], axis=1)
    pieces = [kv_same] + [None] * (seq_count - 1)
    for mask in range(seq_count - 1, 1, -1):
        pieces[mask] = seq_send(kv_other if mask & 1 else kv_same, mask)
    pieces[1] = seq_send(jnp.concatenate(other, axis=1), 1)

    gate_columns = -(-2 * expert_count // LANES) * LANES
    loaded = [
        residual,
        norm_gain[None, :],
        out_weight,
        gate_weight.transpose(0, 2, 1).reshape(local * hidden_units, width),
        up_weight.transpose(0, 2, 1).reshape(local * hidden_units, width),
        down_weight.reshape(local * hidden_units, width),
    ]
    shapes = [jax.ShapeDtypeStruct(a.shape, a.dtype) for a in loaded]
    shapes[0] = jax.ShapeDtypeStruct((share, width), residual.dtype)
    shapes.append(jax.ShapeDtypeStruct((1, seq_count * tok_rows), jnp.int32))
    shapes.append(jax.ShapeDtypeStruct((share, gate_columns), bf16))
    residual_rows, gain, out_proj, gate_t, up_t, down, key_pos, gates = call(
        functools.partial(load_kernel, seq_count, exp_count, expert_count),
        tuple(shapes),
        [SMEM, VMEM, VMEM] + [HBM] * len(loaded),
        24,
        [
            pltpu.VMEM((tok_rows, gate_columns), f32),
            pltpu.SemaphoreType.DMA((len(loaded),)),
        ],
    )(block_picks, routes.T, route_gates.T, *[pltpu.with_memory_space_constraint(a, HBM) for a in loaded])

    half_shape = jax.ShapeDtypeStruct((tok_rows, half_width), bf16)
    attended, partner_attended = call(
        functools.partial(attention_kernel, seq_count),
        (half_shape, half_shape),
        [VMEM] * (2 + seq_count),
        32,
    )(key_pos, half_of(queries, core), *pieces)
    other_attended = seq_send(partner_attended, 1)

    projected = call(
        functools.partial(project_kernel, exp_count),
        (jax.ShapeDtypeStruct((share, width), f32),)
        + (jax.ShapeDtypeStruct((share, width), bf16),) * (exp_count - 1),
        [VMEM] * 3,
        16,
    )(attended, other_attended, out_proj)
    received = [exp_send(projected[r], r) for r in range(1, exp_count)]

    hidden, own_rows = call(
        functools.partial(norm_kernel, exp_count),
        (
            jax.ShapeDtypeStruct((share, width), f32),
            jax.ShapeDtypeStruct((share, width + gate_columns), bf16),
        ),
        [VMEM] * (exp_count + 3),
        8,
    )(projected[0], *received, residual_rows, gain, gates)

    far = [1 << b for b in range(1, (seq_count - 1).bit_length())]
    turned = far[len(far) // 2 :] + far[: len(far) // 2]

    def lane_send(a, step):
        pairs = [(i, i ^ (turned[step] if i & 1 else far[step])) for i in range(seq_count)]
        return lax.ppermute(a, "seq", pairs)

    def lane_exp_send(a, even, odd):
        pairs = [
            (i * exp_count + j, i * exp_count + (j ^ (odd if i & 1 else even)))
            for i in range(seq_count)
            for j in range(exp_count)
        ]
        return lax.ppermute(a, ("seq", "exp"), pairs)

    def mlp(arrays):
        outs = call(
            functools.partial(expert_kernel, expert_count, local, len(arrays)),
            tuple(jax.ShapeDtypeStruct(a.shape[:2] + (width,), bf16) for a in arrays),
            [VMEM] * (len(arrays) + 3),
            32,
        )(*arrays, gate_t, up_t, down)
        return list(outs)

    if exp_count == 4:
        groups = [(0, 0), (1, 2), (3, 3)]
    else:
        groups = [(r, r) for r in range(exp_count)]
    own_rows = own_rows[None]
    bases = []
    for even, odd in groups:
        base = own_rows
        if even != odd:
            base = join(own_rows, seq_send(own_rows, 1))
        bases.append(lane_exp_send(base, even, odd) if even or odd else base)
    mixture = 0.0
    for at, (even, odd) in enumerate(groups):
        whole = bases[at]
        for step in range(len(far)):
            arrived = lane_send(whole, step)
            if step + 1 < len(far):
                whole = join(whole, arrived)
        mine = [whole, arrived]
        other = [seq_send(a, 1) for a in mine]
        if even != odd:
            sums = mlp(other)
            parts = [seq_send(sums[i], 1) for i in (1, 0)][::-1]
            sums = mlp(mine)
        else:
            sums = mlp(other + mine)
            parts = [seq_send(sums[i], 1) for i in (1, 0)][::-1]
            sums = sums[2:]
        (sent,) = plus(sums[1], parts[1])
        (kept,) = plus(sums[0], parts[0])
        for step in reversed(range(len(far))):
            arrived = lane_send(sent, step)
            if step:
                kept, sent = plus(kept, arrived, 2)
            else:
                (kept,) = plus(kept, arrived)
        if even or odd:
            kept = lane_exp_send(kept, even, odd)
        mixture = mixture + kept[0].astype(f32)
        if even != odd:
            mixture = mixture + seq_send(kept[1], 1).astype(f32)
    return (hidden + mixture).astype(bf16)


def solution(mesh):
    placed = (
        P("seq", "exp"),
        P("seq", "exp"),
        P("seq", "exp"),
        P("seq", None),
        P("exp", None),
        P(),
        P("seq", None, "exp"),
        P("seq", None, "exp"),
        P("seq", "exp", None),
        P("seq", None),
        P("seq", None),
        P(),
    )

    return jax.shard_map(
        per_device, mesh=mesh, in_specs=placed, out_specs=P(("seq", "exp"), None), check_vma=False
    )
```

```python
import functools

import jax
import jax.numpy as jnp
from jax import lax
from jax.experimental import pallas as pl
from jax.experimental.pallas import tpu as pltpu
from jax.sharding import PartitionSpec as P


HD = 128
BLK = 512
LANES = 128
MIB = 1 << 20
VMEM = pltpu.MemorySpace.VMEM
SMEM = pltpu.MemorySpace.SMEM
HBM = pltpu.MemorySpace.HBM


def call(kernel, out_shape, in_spaces, limit, scratch=()):
    specs = [pl.BlockSpec(memory_space=s) for s in in_spaces]
    return pl.pallas_call(
        kernel,
        out_shape=out_shape,
        in_specs=specs,
        out_specs=jax.tree.map(lambda _: pl.BlockSpec(memory_space=VMEM), out_shape),
        scratch_shapes=list(scratch),
        compiler_params=pltpu.CompilerParams(vmem_limit_bytes=limit * MIB),
    )


def xor_swap(count, mask):
    return [(i, i ^ mask) for i in range(count)]


def load_kernel(seq_count, exp_count, expert_count, picks_ref, routes_ref, gates_ref, *refs):
    copied = (len(refs) - 4) // 2
    sources, targets = refs[:copied], refs[copied : 2 * copied]
    key_out, gates_out, turned, sems = refs[2 * copied :]
    seq_index, exp_index = lax.axis_index("seq"), lax.axis_index("exp")
    top, rows = routes_ref.shape
    share = rows // exp_count
    here = pl.ds(pl.multiple_of(exp_index * share, share), share)
    copies = []
    for i in range(copied):
        source = sources[i].at[here] if i == 0 else sources[i]
        copies.append(pltpu.make_async_copy(source, targets[i], sems.at[i]))
        copies[-1].start()

    block = seq_index * rows // BLK
    lane = lax.broadcasted_iota(jnp.int32, (1, rows), 1)
    for mask in range(seq_count):
        group = seq_index ^ mask
        key_block = group * rows // BLK
        seen = picks_ref[block, 0] == key_block
        for j in range(1, picks_ref.shape[1]):
            seen = seen | (picks_ref[block, j] == key_block)
        key_out[:, mask * rows : (mask + 1) * rows] = lane + jnp.where(seen, group * rows, 1 << 30)

    width = gates_out.shape[1]
    line = lax.broadcasted_iota(jnp.int32, (width, rows), 0)
    expert = jnp.where(line < expert_count, line, line - expert_count)
    value = jnp.zeros((width, rows), jnp.float32)
    for k in range(top):
        hit = expert == routes_ref[k : k + 1, :]
        value = value + jnp.where(hit, gates_ref[k : k + 1, :], 0.0)
    high = value.astype(jnp.bfloat16).astype(jnp.float32)
    turned[...] = jnp.where(line < expert_count, high, value - high).T
    gates_out[...] = turned[here, :].astype(jnp.bfloat16)
    for copy in copies:
        copy.wait()


def attention_kernel(count, key_ref, own_ref, *refs):
    pieces, (own_out, partner_out) = refs[:count], refs[count:]
    seq_index = lax.axis_index("seq")
    rows, width = own_ref.shape
    key_pos = key_ref[...]
    line = lax.broadcasted_iota(jnp.int32, (rows, 1), 0)
    query_pos = jnp.concatenate(
        [line + seq_index * rows, line + (seq_index ^ 1) * rows], axis=0
    )
    allowed = key_pos <= query_pos
    for first in range(0, width, HD):
        q = jnp.concatenate(
            [
                own_ref[:, first : first + HD],
                pieces[1][:, 2 * width + first : 2 * width + first + HD],
            ],
            axis=0,
        )
        k = jnp.concatenate([p[:, first : first + HD] for p in pieces], axis=0)
        v = jnp.concatenate(
            [p[:, width + first : width + first + HD] for p in pieces], axis=0
        )
        scores = lax.dot_general(
            q, k, (((1,), (1,)), ((), ())), preferred_element_type=jnp.float32
        ) * (HD ** -0.5)
        scores = jnp.where(allowed, scores, -1e30)
        peak = jnp.max(scores, axis=1, keepdims=True)
        expo = jnp.where(allowed, jnp.exp(scores - peak), 0.0)
        total = jnp.sum(expo, axis=1, keepdims=True)
        mixed = jnp.dot(expo.astype(jnp.bfloat16), v, preferred_element_type=jnp.float32) / total
        mixed = mixed.astype(jnp.bfloat16)
        own_out[:, first : first + HD] = mixed[:rows]
        partner_out[:, first : first + HD] = mixed[rows:]


def project_kernel(exp_count, mine_ref, other_ref, weight_ref, own_out, *outs):
    rows, width = mine_ref.shape
    share = rows // exp_count
    exp_index = lax.axis_index("exp")
    half = lax.axis_index("seq") & 1

    def turned(ref):
        parts = []
        for r in range(exp_count):
            first = pl.multiple_of((exp_index ^ r) * share, share)
            parts.append(ref[pl.ds(first, share), :])
        return jnp.concatenate(parts, axis=0)

    first = pl.multiple_of(half * width, width)
    last = pl.multiple_of((1 - half) * width, width)
    result = jnp.dot(
        turned(mine_ref), weight_ref[pl.ds(first, width), :], preferred_element_type=jnp.float32
    ) + jnp.dot(
        turned(other_ref), weight_ref[pl.ds(last, width), :], preferred_element_type=jnp.float32
    )
    own_out[...] = result[:share]
    for r in range(1, exp_count):
        outs[r - 1][...] = result[r * share : (r + 1) * share].astype(jnp.bfloat16)


def norm_kernel(exp_count, own_ref, *refs):
    received = refs[: exp_count - 1]
    residual_ref, gain_ref, gates_ref, hidden_out, rows_out = refs[exp_count - 1 :]
    width = own_ref.shape[1]
    projected = own_ref[...]
    for r in received:
        projected = projected + r[...].astype(jnp.float32)
    hidden = residual_ref[...].astype(jnp.float32) + projected
    mean_square = jnp.mean(hidden * hidden, axis=-1, keepdims=True)
    hidden_out[...] = hidden
    rows_out[:, :width] = (hidden * lax.rsqrt(mean_square + 1e-06) * gain_ref[...]).astype(
        jnp.bfloat16
    )
    rows_out[:, width:] = gates_ref[...]


def expert_kernel(expert_count, local, arrays, *refs):
    pieces = refs[:arrays]
    gate_ref, up_ref, down_ref = refs[arrays : arrays + 3]
    outs = refs[arrays + 3 :]
    rows = pieces[0].shape[1]
    inner_width, width = down_ref.shape
    hidden_units = inner_width // local
    places = [(p, i) for p in pieces for i in range(p.shape[0])]
    tokens = jnp.concatenate([p[i, :, :width] for p, i in places], axis=0)
    gates = jnp.concatenate([p[i, :, width:] for p, i in places], axis=0)
    gates = gates.astype(jnp.float32)
    line = lax.broadcasted_iota(jnp.int32, (1, gates.shape[1]), 1)
    column = lax.broadcasted_iota(jnp.int32, (1, inner_width), 1)
    scale = jnp.zeros((gates.shape[0], inner_width), jnp.float32)
    for e in range(local):
        expert = lax.axis_index("seq") * local + e
        chosen = (line == expert) | (line == expert + expert_count)
        value = jnp.sum(jnp.where(chosen, gates, 0.0), axis=1, keepdims=True)
        here = (column >= e * hidden_units) & (column < (e + 1) * hidden_units)
        scale = jnp.where(here, value, scale)
    turn = (((1,), (1,)), ((), ()))
    gate = lax.dot_general(tokens, gate_ref[...], turn, preferred_element_type=jnp.float32)
    up = lax.dot_general(tokens, up_ref[...], turn, preferred_element_type=jnp.float32)
    inner = (gate / (1.0 + jnp.exp(-gate)) * up * scale).astype(jnp.bfloat16)
    result = jnp.dot(inner, down_ref[...], preferred_element_type=jnp.float32)
    at = 0
    for out in outs:
        for i in range(out.shape[0]):
            out[i] = result[at : at + rows].astype(jnp.bfloat16)
            at += rows


def join_kernel(a_ref, b_ref, out_ref):
    out_ref[: a_ref.shape[0]] = a_ref[...]
    out_ref[a_ref.shape[0] :] = b_ref[...]


def join(a, b):
    shape = jax.ShapeDtypeStruct((a.shape[0] + b.shape[0],) + a.shape[1:], a.dtype)
    return call(join_kernel, shape, [VMEM] * 2, 8)(a, b)


def plus_kernel(parts, *refs):
    more, outs = refs[parts:-parts], refs[-parts:]
    at = 0
    for own, out in zip(refs, outs):
        value = own[...].astype(jnp.float32)
        for whole in more:
            value = value + whole[at : at + own.shape[0]].astype(jnp.float32)
        out[...] = value.astype(out.dtype)
        at += own.shape[0]


def plus(owns, *more):
    shapes = tuple(jax.ShapeDtypeStruct(a.shape, a.dtype) for a in owns)
    kernel = functools.partial(plus_kernel, len(owns))
    return call(kernel, shapes, [VMEM] * (len(owns) + len(more)), 8)(*owns, *more)


def final_kernel(hidden_ref, *refs):
    value = hidden_ref[...]
    for r in refs[:-1]:
        value = value + r[0].astype(jnp.float32)
    refs[-1][...] = value.astype(refs[-1].dtype)


def per_device(
    queries,
    key_rows,
    value_rows,
    residual,
    out_weight,
    norm_gain,
    gate_weight,
    up_weight,
    down_weight,
    routes,
    route_gates,
    block_picks,
):
    seq_count = lax.axis_size("seq")
    exp_count = lax.axis_size("exp")
    seq_index = lax.axis_index("seq")
    tok_rows, head_width = queries.shape
    width = residual.shape[1]
    share = tok_rows // exp_count
    local, _, hidden_units = gate_weight.shape
    expert_count = local * seq_count
    half_width = head_width // 2
    core = seq_index & 1
    bf16, f32 = jnp.bfloat16, jnp.float32

    def seq_send(a, mask):
        return lax.ppermute(a, "seq", xor_swap(seq_count, mask))

    def exp_send(a, by):
        return lax.ppermute(a, "exp", xor_swap(exp_count, by))

    def half_of(a, which):
        return lax.dynamic_slice_in_dim(a, which * half_width, half_width, 1)

    kv_same = jnp.concatenate([half_of(key_rows, core), half_of(value_rows, core)], axis=1)
    other = [half_of(a, 1 - core) for a in (key_rows, value_rows, queries)]
    kv_other = jnp.concatenate(other[:2], axis=1)
    pieces = [kv_same] + [None] * (seq_count - 1)
    for mask in range(seq_count - 1, 1, -1):
        pieces[mask] = seq_send(kv_other if mask & 1 else kv_same, mask)
    pieces[1] = seq_send(jnp.concatenate(other, axis=1), 1)

    gate_columns = -(-2 * expert_count // LANES) * LANES
    loaded = [
        residual,
        norm_gain[None, :],
        out_weight,
        gate_weight.transpose(0, 2, 1).reshape(local * hidden_units, width),
        up_weight.transpose(0, 2, 1).reshape(local * hidden_units, width),
        down_weight.reshape(local * hidden_units, width),
    ]
    shapes = [jax.ShapeDtypeStruct(a.shape, a.dtype) for a in loaded]
    shapes[0] = jax.ShapeDtypeStruct((share, width), residual.dtype)
    shapes.append(jax.ShapeDtypeStruct((1, seq_count * tok_rows), jnp.int32))
    shapes.append(jax.ShapeDtypeStruct((share, gate_columns), bf16))
    residual_rows, gain, out_proj, gate_t, up_t, down, key_pos, gates = call(
        functools.partial(load_kernel, seq_count, exp_count, expert_count),
        tuple(shapes),
        [SMEM, VMEM, VMEM] + [HBM] * len(loaded),
        24,
        [
            pltpu.VMEM((tok_rows, gate_columns), f32),
            pltpu.SemaphoreType.DMA((len(loaded),)),
        ],
    )(block_picks, routes.T, route_gates.T, *[pltpu.with_memory_space_constraint(a, HBM) for a in loaded])

    half_shape = jax.ShapeDtypeStruct((tok_rows, half_width), bf16)
    attended, partner_attended = call(
        functools.partial(attention_kernel, seq_count),
        (half_shape, half_shape),
        [VMEM] * (2 + seq_count),
        32,
    )(key_pos, half_of(queries, core), *pieces)
    other_attended = seq_send(partner_attended, 1)

    projected = call(
        functools.partial(project_kernel, exp_count),
        (jax.ShapeDtypeStruct((share, width), f32),)
        + (jax.ShapeDtypeStruct((share, width), bf16),) * (exp_count - 1),
        [VMEM] * 3,
        16,
    )(attended, other_attended, out_proj)
    received = [exp_send(projected[r], r) for r in range(1, exp_count)]

    hidden, own_rows = call(
        functools.partial(norm_kernel, exp_count),
        (
            jax.ShapeDtypeStruct((share, width), f32),
            jax.ShapeDtypeStruct((share, width + gate_columns), bf16),
        ),
        [VMEM] * (exp_count + 3),
        8,
    )(projected[0], *received, residual_rows, gain, gates)

    far = [1 << b for b in range(1, (seq_count - 1).bit_length())]
    turned = far[len(far) // 2 :] + far[: len(far) // 2]

    def lane_send(a, step):
        pairs = [(i, i ^ (turned[step] if i & 1 else far[step])) for i in range(seq_count)]
        return lax.ppermute(a, "seq", pairs)

    def gather(own):
        for step in range(len(far)):
            own = join(own, lane_send(own, step))
        return own

    def mlp(mine):
        other = seq_send(mine, 1)
        units = mine.shape[0]
        shapes = [(units,), (units // 2,), (units // 2,)]
        outs = call(
            functools.partial(expert_kernel, expert_count, local, 2),
            tuple(jax.ShapeDtypeStruct(n + (share, width), bf16) for n in shapes),
            [VMEM] * 5,
            32,
        )(other, mine, gate_t, up_t, down)
        return list(outs[1:]), seq_send(outs[0], 1)

    bases, wholes, sums = {}, {}, {}
    for r in range(exp_count):
        if r == 1:
            wholes[r] = exp_send(wholes[0], 1)
        else:
            if r == 0:
                bases[r] = own_rows[None]
            elif r & 1:
                bases[r] = exp_send(bases[r - 1], 1)
            else:
                bases[r] = exp_send(bases[0], r)
            wholes[r] = gather(bases[r])
        sums[r] = mlp(wholes[r])
    shares = []
    for r in range(exp_count):
        parts, arrived = sums[r]
        kept, sent = plus(parts, arrived)
        for step in reversed(range(len(far))):
            arrived = lane_send(sent, step)
            middle = kept.shape[0] // 2
            halves = [kept[:middle], kept[middle:]] if step else [kept]
            kept, *rest = plus(halves, arrived)
            sent = rest[0] if rest else None
        shares.append(exp_send(kept, r) if r else kept)
    return call(
        final_kernel, jax.ShapeDtypeStruct((share, width), bf16), [VMEM] * (1 + len(shares)), 8
    )(hidden, *shares)


def solution(mesh):
    placed = (
        P("seq", "exp"),
        P("seq", "exp"),
        P("seq", "exp"),
        P("seq", None),
        P("exp", None),
        P(),
        P("seq", None, "exp"),
        P("seq", None, "exp"),
        P("seq", "exp", None),
        P("seq", None),
        P("seq", None),
        P(),
    )

    return jax.shard_map(
        per_device, mesh=mesh, in_specs=placed, out_specs=P(("seq", "exp"), None), check_vma=False
    )
```

```python
import functools

import jax
import jax.numpy as jnp
from jax import lax
from jax.experimental import pallas as pl
from jax.experimental.pallas import tpu as pltpu
from jax.sharding import PartitionSpec as P


HD = 128
BLK = 512
LANES = 128
MIB = 1 << 20
VMEM = pltpu.MemorySpace.VMEM
SMEM = pltpu.MemorySpace.SMEM
HBM = pltpu.MemorySpace.HBM


def call(kernel, out_shape, in_spaces, limit, scratch=()):
    specs = [pl.BlockSpec(memory_space=s) for s in in_spaces]
    return pl.pallas_call(
        kernel,
        out_shape=out_shape,
        in_specs=specs,
        out_specs=jax.tree.map(lambda _: pl.BlockSpec(memory_space=VMEM), out_shape),
        scratch_shapes=list(scratch),
        compiler_params=pltpu.CompilerParams(vmem_limit_bytes=limit * MIB),
    )


def xor_swap(count, mask):
    return [(i, i ^ mask) for i in range(count)]


def fetch_kernel(*refs):
    count = len(refs) // 2
    sems = refs[2 * count]
    copies = [pltpu.make_async_copy(refs[i], refs[count + i], sems.at[i]) for i in range(count)]
    for copy in copies:
        copy.start()
    for copy in copies:
        copy.wait()


def load_kernel(seq_count, exp_count, expert_count, picks_ref, routes_ref, gates_ref, *refs):
    copied = (len(refs) - 4) // 2
    sources, targets = refs[:copied], refs[copied : 2 * copied]
    key_out, gates_out, turned, sems = refs[2 * copied :]
    seq_index, exp_index = lax.axis_index("seq"), lax.axis_index("exp")
    top, rows = routes_ref.shape
    share = rows // exp_count
    here = pl.ds(pl.multiple_of(exp_index * share, share), share)
    copies = []
    for i in range(copied):
        source = sources[i].at[here] if i == 0 else sources[i]
        copies.append(pltpu.make_async_copy(source, targets[i], sems.at[i]))
        copies[-1].start()

    block = seq_index * rows // BLK
    lane = lax.broadcasted_iota(jnp.int32, (1, rows), 1)
    for mask in range(seq_count):
        group = seq_index ^ mask
        key_block = group * rows // BLK
        seen = picks_ref[block, 0] == key_block
        for j in range(1, picks_ref.shape[1]):
            seen = seen | (picks_ref[block, j] == key_block)
        key_out[:, mask * rows : (mask + 1) * rows] = lane + jnp.where(seen, group * rows, 1 << 30)

    width = gates_out.shape[1]
    line = lax.broadcasted_iota(jnp.int32, (width, rows), 0)
    expert = jnp.where(line < expert_count, line, line - expert_count)
    value = jnp.zeros((width, rows), jnp.float32)
    for k in range(top):
        hit = expert == routes_ref[k : k + 1, :]
        value = value + jnp.where(hit, gates_ref[k : k + 1, :], 0.0)
    high = value.astype(jnp.bfloat16).astype(jnp.float32)
    turned[...] = jnp.where(line < expert_count, high, value - high).T
    gates_out[...] = turned[here, :].astype(jnp.bfloat16)
    for copy in copies:
        copy.wait()


def attention_kernel(count, key_ref, own_ref, *refs):
    pieces, (own_out, partner_out) = refs[:count], refs[count:]
    seq_index = lax.axis_index("seq")
    rows, width = own_ref.shape
    key_pos = key_ref[...]
    line = lax.broadcasted_iota(jnp.int32, (rows, 1), 0)
    query_pos = jnp.concatenate(
        [line + seq_index * rows, line + (seq_index ^ 1) * rows], axis=0
    )
    allowed = key_pos <= query_pos
    for first in range(0, width, HD):
        q = jnp.concatenate(
            [
                own_ref[:, first : first + HD],
                pieces[1][:, 2 * width + first : 2 * width + first + HD],
            ],
            axis=0,
        )
        k = jnp.concatenate([p[:, first : first + HD] for p in pieces], axis=0)
        v = jnp.concatenate(
            [p[:, width + first : width + first + HD] for p in pieces], axis=0
        )
        scores = lax.dot_general(
            q, k, (((1,), (1,)), ((), ())), preferred_element_type=jnp.float32
        ) * (HD ** -0.5)
        scores = jnp.where(allowed, scores, -1e30)
        peak = jnp.max(scores, axis=1, keepdims=True)
        expo = jnp.where(allowed, jnp.exp(scores - peak), 0.0)
        total = jnp.sum(expo, axis=1, keepdims=True)
        mixed = jnp.dot(expo.astype(jnp.bfloat16), v, preferred_element_type=jnp.float32) / total
        mixed = mixed.astype(jnp.bfloat16)
        own_out[:, first : first + HD] = mixed[:rows]
        partner_out[:, first : first + HD] = mixed[rows:]


def project_kernel(exp_count, mine_ref, other_ref, weight_ref, own_out, *outs):
    rows, width = mine_ref.shape
    share = rows // exp_count
    exp_index = lax.axis_index("exp")
    half = lax.axis_index("seq") & 1

    def turned(ref):
        parts = []
        for r in range(exp_count):
            first = pl.multiple_of((exp_index ^ r) * share, share)
            parts.append(ref[pl.ds(first, share), :])
        return jnp.concatenate(parts, axis=0)

    first = pl.multiple_of(half * width, width)
    last = pl.multiple_of((1 - half) * width, width)
    result = jnp.dot(
        turned(mine_ref), weight_ref[pl.ds(first, width), :], preferred_element_type=jnp.float32
    ) + jnp.dot(
        turned(other_ref), weight_ref[pl.ds(last, width), :], preferred_element_type=jnp.float32
    )
    own_out[...] = result[:share]
    for r in range(1, exp_count):
        outs[r - 1][...] = result[r * share : (r + 1) * share].astype(jnp.bfloat16)


def norm_kernel(exp_count, own_ref, *refs):
    received = refs[: exp_count - 1]
    residual_ref, gain_ref, gates_ref, hidden_out, rows_out = refs[exp_count - 1 :]
    width = own_ref.shape[1]
    projected = own_ref[...]
    for r in received:
        projected = projected + r[...].astype(jnp.float32)
    hidden = residual_ref[...].astype(jnp.float32) + projected
    mean_square = jnp.mean(hidden * hidden, axis=-1, keepdims=True)
    hidden_out[...] = hidden
    rows_out[:, :width] = (hidden * lax.rsqrt(mean_square + 1e-06) * gain_ref[...]).astype(
        jnp.bfloat16
    )
    rows_out[:, width:] = gates_ref[...]


def expert_kernel(expert_count, local, arrays, *refs):
    pieces = refs[:arrays]
    gate_ref, up_ref, down_ref = refs[arrays : arrays + 3]
    outs = refs[arrays + 3 :]
    rows = pieces[0].shape[1]
    inner_width, width = down_ref.shape
    hidden_units = inner_width // local
    places = [(p, i) for p in pieces for i in range(p.shape[0])]
    tokens = jnp.concatenate([p[i, :, :width] for p, i in places], axis=0)
    gates = jnp.concatenate([p[i, :, width:] for p, i in places], axis=0)
    gates = gates.astype(jnp.float32)
    line = lax.broadcasted_iota(jnp.int32, (1, gates.shape[1]), 1)
    column = lax.broadcasted_iota(jnp.int32, (1, inner_width), 1)
    scale = jnp.zeros((gates.shape[0], inner_width), jnp.float32)
    for e in range(local):
        expert = lax.axis_index("seq") * local + e
        chosen = (line == expert) | (line == expert + expert_count)
        value = jnp.sum(jnp.where(chosen, gates, 0.0), axis=1, keepdims=True)
        here = (column >= e * hidden_units) & (column < (e + 1) * hidden_units)
        scale = jnp.where(here, value, scale)
    turn = (((1,), (1,)), ((), ()))
    gate = lax.dot_general(tokens, gate_ref[...], turn, preferred_element_type=jnp.float32)
    up = lax.dot_general(tokens, up_ref[...], turn, preferred_element_type=jnp.float32)
    inner = (gate / (1.0 + jnp.exp(-gate)) * up * scale).astype(jnp.bfloat16)
    result = jnp.dot(inner, down_ref[...], preferred_element_type=jnp.float32)
    at = 0
    for out in outs:
        for i in range(out.shape[0]):
            out[i] = result[at : at + rows].astype(jnp.bfloat16)
            at += rows


def join_kernel(a_ref, b_ref, out_ref):
    out_ref[: a_ref.shape[0]] = a_ref[...]
    out_ref[a_ref.shape[0] :] = b_ref[...]


def join(a, b):
    shape = jax.ShapeDtypeStruct((a.shape[0] + b.shape[0],) + a.shape[1:], a.dtype)
    return call(join_kernel, shape, [VMEM] * 2, 8)(a, b)


def plus_kernel(parts, *refs):
    more, outs = refs[parts:-parts], refs[-parts:]
    at = 0
    for own, out in zip(refs, outs):
        value = own[...].astype(jnp.float32)
        for whole in more:
            value = value + whole[at : at + own.shape[0]].astype(jnp.float32)
        out[...] = value.astype(out.dtype)
        at += own.shape[0]


def plus(owns, *more):
    shapes = tuple(jax.ShapeDtypeStruct(a.shape, a.dtype) for a in owns)
    kernel = functools.partial(plus_kernel, len(owns))
    return call(kernel, shapes, [VMEM] * (len(owns) + len(more)), 8)(*owns, *more)


def final_kernel(hidden_ref, *refs):
    value = hidden_ref[...]
    for r in refs[:-1]:
        value = value + r[0].astype(jnp.float32)
    refs[-1][...] = value.astype(refs[-1].dtype)


def per_device(
    queries,
    key_rows,
    value_rows,
    residual,
    out_weight,
    norm_gain,
    gate_weight,
    up_weight,
    down_weight,
    routes,
    route_gates,
    block_picks,
):
    seq_count = lax.axis_size("seq")
    exp_count = lax.axis_size("exp")
    seq_index = lax.axis_index("seq")
    tok_rows, head_width = queries.shape
    width = residual.shape[1]
    share = tok_rows // exp_count
    local, _, hidden_units = gate_weight.shape
    expert_count = local * seq_count
    half_width = head_width // 2
    core = seq_index & 1
    bf16, f32 = jnp.bfloat16, jnp.float32

    def seq_send(a, mask):
        return lax.ppermute(a, "seq", xor_swap(seq_count, mask))

    def exp_send(a, by):
        return lax.ppermute(a, "exp", xor_swap(exp_count, by))

    def half_of(a, which):
        return lax.dynamic_slice_in_dim(a, which * half_width, half_width, 1)

    kv_same = jnp.concatenate([half_of(key_rows, core), half_of(value_rows, core)], axis=1)
    other = [half_of(a, 1 - core) for a in (key_rows, value_rows, queries)]
    kv_other = jnp.concatenate(other[:2], axis=1)
    pieces = [kv_same] + [None] * (seq_count - 1)
    for mask in range(seq_count - 1, 1, -1):
        pieces[mask] = seq_send(kv_other if mask & 1 else kv_same, mask)
    pieces[1] = seq_send(jnp.concatenate(other, axis=1), 1)

    gate_columns = -(-2 * expert_count // LANES) * LANES
    loaded = [
        residual,
        norm_gain[None, :],
        out_weight,
        gate_weight.transpose(0, 2, 1).reshape(local * hidden_units, width),
        up_weight.transpose(0, 2, 1).reshape(local * hidden_units, width),
        down_weight.reshape(local * hidden_units, width),
    ]
    near = loaded[:3]
    shapes = [jax.ShapeDtypeStruct(a.shape, a.dtype) for a in near]
    shapes[0] = jax.ShapeDtypeStruct((share, width), residual.dtype)
    shapes.append(jax.ShapeDtypeStruct((1, seq_count * tok_rows), jnp.int32))
    shapes.append(jax.ShapeDtypeStruct((share, gate_columns), bf16))
    weights = [pltpu.with_memory_space_constraint(a, HBM) for a in loaded[3:]]
    gate_t, up_t, down = call(
        fetch_kernel,
        tuple(jax.ShapeDtypeStruct(a.shape, a.dtype) for a in weights),
        [HBM] * len(weights),
        24,
        [pltpu.SemaphoreType.DMA((len(weights),))],
    )(*weights)
    residual_rows, gain, out_proj, key_pos, gates = call(
        functools.partial(load_kernel, seq_count, exp_count, expert_count),
        tuple(shapes),
        [SMEM, VMEM, VMEM] + [HBM] * len(near),
        24,
        [
            pltpu.VMEM((tok_rows, gate_columns), f32),
            pltpu.SemaphoreType.DMA((len(near),)),
        ],
    )(block_picks, routes.T, route_gates.T, *[pltpu.with_memory_space_constraint(a, HBM) for a in near])

    half_shape = jax.ShapeDtypeStruct((tok_rows, half_width), bf16)
    attended, partner_attended = call(
        functools.partial(attention_kernel, seq_count),
        (half_shape, half_shape),
        [VMEM] * (2 + seq_count),
        32,
    )(key_pos, half_of(queries, core), *pieces)
    other_attended = seq_send(partner_attended, 1)

    projected = call(
        functools.partial(project_kernel, exp_count),
        (jax.ShapeDtypeStruct((share, width), f32),)
        + (jax.ShapeDtypeStruct((share, width), bf16),) * (exp_count - 1),
        [VMEM] * 3,
        16,
    )(attended, other_attended, out_proj)
    received = [exp_send(projected[r], r) for r in range(1, exp_count)]

    hidden, own_rows = call(
        functools.partial(norm_kernel, exp_count),
        (
            jax.ShapeDtypeStruct((share, width), f32),
            jax.ShapeDtypeStruct((share, width + gate_columns), bf16),
        ),
        [VMEM] * (exp_count + 3),
        8,
    )(projected[0], *received, residual_rows, gain, gates)

    far = [1 << b for b in range(1, (seq_count - 1).bit_length())]
    turned = far[len(far) // 2 :] + far[: len(far) // 2]

    def lane_send(a, step):
        pairs = [(i, i ^ (turned[step] if i & 1 else far[step])) for i in range(seq_count)]
        return lax.ppermute(a, "seq", pairs)

    def gather(own):
        for step in range(len(far)):
            own = join(own, lane_send(own, step))
        return own

    def mlp(mine):
        other = seq_send(mine, 1)
        units = mine.shape[0]
        shapes = [(units,), (units // 2,), (units // 2,)]
        outs = call(
            functools.partial(expert_kernel, expert_count, local, 2),
            tuple(jax.ShapeDtypeStruct(n + (share, width), bf16) for n in shapes),
            [VMEM] * 5,
            32,
        )(other, mine, gate_t, up_t, down)
        return list(outs[1:]), seq_send(outs[0], 1)

    bases, wholes, sums = {}, {}, {}
    for r in range(exp_count):
        if r == 1:
            wholes[r] = exp_send(wholes[0], 1)
        else:
            if r == 0:
                bases[r] = own_rows[None]
            elif r & 1:
                bases[r] = exp_send(bases[r - 1], 1)
            else:
                bases[r] = exp_send(bases[0], r)
            wholes[r] = gather(bases[r])
        sums[r] = mlp(wholes[r])
    shares = []
    for r in range(exp_count):
        parts, arrived = sums[r]
        kept, sent = plus(parts, arrived)
        for step in reversed(range(len(far))):
            arrived = lane_send(sent, step)
            middle = kept.shape[0] // 2
            halves = [kept[:middle], kept[middle:]] if step else [kept]
            kept, *rest = plus(halves, arrived)
            sent = rest[0] if rest else None
        shares.append(exp_send(kept, r) if r else kept)
    return call(
        final_kernel, jax.ShapeDtypeStruct((share, width), bf16), [VMEM] * (1 + len(shares)), 8
    )(hidden, *shares)


def solution(mesh):
    placed = (
        P("seq", "exp"),
        P("seq", "exp"),
        P("seq", "exp"),
        P("seq", None),
        P("exp", None),
        P(),
        P("seq", None, "exp"),
        P("seq", None, "exp"),
        P("seq", "exp", None),
        P("seq", None),
        P("seq", None),
        P(),
    )

    return jax.shard_map(
        per_device, mesh=mesh, in_specs=placed, out_specs=P(("seq", "exp"), None), check_vma=False
    )
```
